128 devices in a mesh: rows: 64 (over z, y_hi, x, core), layer: 2 (over y_lo).
Axes of the slice: x: 4, y: 4 (y_hi: 2, y_lo: 2; y = y_hi * 2 + y_lo), z: 4, core: 2. Of those that a mesh axis runs over, the one named last changes fastest.
Arguments:
- gradients: float32 [4096, 32, 2880], P(('layer', 'rows')), parts along dimension 0, may hold values from -6 to 6
- in_basis: bfloat16 [5760, 2880], P(('layer', 'rows')), parts along dimension 0, may hold values from -0.109375 to 0.109375
- out_basis: bfloat16 [4096, 2048], P(('layer', 'rows')), parts along dimension 0, may hold values from -0.125 to 0.125
- eigen_seeds: int32 [5760, 2048], P(('layer', 'rows')), parts along dimension 0, may hold values from 0 to 63
Outputs:
- precond: float32 [4096, 92160], P('layer', 'rows'), parts along dimension 0
The draws below stay inside these ranges and needn't reach their ends.
There are 2 independent parts, one for each index of `layer`. The reference program is written for one: setup_inputs(seed, part) draws one part's arguments, and reference() takes and returns one part's arrays. A program takes and returns all parts, laid end to end along the dimension named above; each array names one. Nothing has to cross between parts.
All inputs are finite; a program needn't handle non-finite values.
Results may differ from the reference program's by a relative error of at most 0.0041.
Values may be sent and summed in bfloat16 or wider, within the bound.
A program may use at most 192 MiB of HBM per device.

```python
import jax
import jax.numpy as jnp

DOUT = 2048
DIN = 2880
NG = 32


def touch_ends(entries, rng, least, top_value):
    longest = entries.shape.index(max(entries.shape))
    spots = []
    for shift in (0, 1):
        where = [jax.random.randint(jax.random.fold_in(rng, axis), (), 0, length) for axis, length in enumerate(entries.shape)]
        where[longest] = (where[longest] + shift) % entries.shape[longest]
        spots.append(tuple(where))
    return entries.at[spots[0]].set(least).at[spots[1]].set(top_value)


def steps_of(stream_key, extent, split, smallest, largest):
    def one(position, blocks):
        draws = jax.random.uniform(jax.random.fold_in(jax.random.fold_in(stream_key, 6), position), (blocks,), jnp.float32, smallest / len(split), largest / len(split))
        return jnp.repeat(jnp.exp(draws), extent[position] // blocks).reshape((-1,) + (1,) * (len(extent) - position - 1))

    factor_of = one(*split[0])
    for cut in split[1:]:
        factor_of = factor_of * one(*cut)
    return factor_of


def centred(key, dims, scale, most, shards=(), dtype=jnp.bfloat16):
    factor_of = steps_of(key, dims, shards, -0.22, 0.18) if shards else 1.0
    drawn = jax.random.normal(key, dims, jnp.float32) * scale * factor_of
    return jnp.minimum(jnp.maximum(drawn, -most), most).astype(dtype)


def setup_inputs(seed: int = 0, part: int = 0) -> dict:
    seeds = jax.random.split(jax.random.key(seed), 5)
    part_splits = jax.random.split(jax.random.fold_in(seeds[4], part), 5)
    return {
        "gradients": centred(part_splits[0], (DOUT, NG, DIN), 1.0, 6.0, ((0, 64),), jnp.float32),
        "in_basis": centred(part_splits[1], (DIN, DIN), DIN ** -0.5, 0.109375, ((0, 64),)),
        "out_basis": centred(part_splits[2], (DOUT, DOUT), DOUT ** -0.5, 0.125, ((0, 64),)),
        "eigen_seeds": touch_ends(jax.random.randint(part_splits[3], (DIN, DOUT), 0, 64), jax.random.fold_in(part_splits[3], 1), 0, 63).astype(jnp.int32),
    }


def reference(gradients, in_basis, out_basis, eigen_seeds):
    grad_low = gradients.astype(jnp.bfloat16).reshape(DOUT * NG, DIN)
    rotated = jnp.dot(grad_low, in_basis, preferred_element_type=jnp.float32).astype(jnp.bfloat16)
    rotated = rotated.reshape(DOUT, NG * DIN)
    both = jnp.dot(out_basis.T, rotated, preferred_element_type=jnp.float32)
    both = both.reshape(DOUT, NG, DIN).transpose(0, 2, 1)
    eigval = jnp.exp2(eigen_seeds.astype(jnp.float32) * 0.125 - 4.0)
    denom = (eigval + 0.1).T
    return (both / denom[:, :, None]).reshape(DOUT, DIN * NG)
```

```python
import functools

import jax
import jax.numpy as jnp
from jax import lax
from jax.experimental import pallas as pl
from jax.experimental.pallas import tpu as pltpu
from jax.sharding import PartitionSpec as P

LANE = 128
F32 = jnp.float32
BF16 = jnp.bfloat16


def up(value, step):
    return -(-value // step) * step


def windows(span, pad, width):
    found = []
    for tile in range(width // span * pad // LANE):
        real = [
            at // pad * span + at % pad
            for at in range(tile * LANE, tile * LANE + LANE)
            if at % pad < span
        ]
        low = real[0] // LANE * LANE
        found.append((low, min(up(real[-1] + 1, LANE), width)))
    return found


def selector(low, high, tile, span, pad):
    source = low + lax.broadcasted_iota(jnp.int32, (high - low, LANE), 0)
    target = tile * LANE + lax.broadcasted_iota(jnp.int32, (high - low, LANE), 1)
    scale = (1 << 21) // pad + 1
    owner = lax.shift_right_logical(target * scale, 21)
    rest = target - owner * pad
    hit = (source == owner * span + rest) & (rest < span)
    return hit.astype(F32).astype(BF16)


def spread(take, put, span, pad, width):
    for tile, (low, high) in enumerate(windows(span, pad, width)):
        chosen = selector(low, high, tile, span, pad)
        moved = jnp.dot(take(low, high), chosen, preferred_element_type=F32)
        put(tile, moved.astype(BF16))


def pad_kernel(span, pad, width, shard_ref, out_ref):
    out_ref[...] = jnp.zeros_like(out_ref)

    def put(tile, value):
        out_ref[0:span, tile * LANE : (tile + 1) * LANE] = value

    spread(lambda low, high: shard_ref[:, low:high], put, span, pad, width)


def pad_shard(shard, pad):
    span, width = shard.shape
    wide = width // span * pad
    return pl.pallas_call(
        functools.partial(pad_kernel, span, pad, width),
        out_shape=jax.ShapeDtypeStruct((pad, wide), BF16),
        in_specs=[pl.BlockSpec(memory_space=pltpu.VMEM)],
        out_specs=pl.BlockSpec(memory_space=pltpu.VMEM),
    )(shard)


def rotate_kernel(rows, grads, span, pad, width, grad_ref, basis_ref, out_ref, raw, column, low_ref, wide_ref, sem):
    @pl.when(pl.program_id(0) == 0)
    def _():
        copy = pltpu.make_async_copy(grad_ref, raw, sem)
        copy.start()
        copy.wait()
        for left in range(0, width, LANE):
            span_now = min(LANE, width - left)
            column[:, 0:span_now] = raw[:, left : left + span_now]
            for g in range(grads):
                picked = column[pl.ds(g, rows, stride=grads), :].astype(BF16)
                low_ref[g * rows : (g + 1) * rows, left : left + span_now] = picked[:, 0:span_now]

        def put(tile, value):
            wide_ref[:, tile * LANE : (tile + 1) * LANE] = value

        spread(lambda low, high: low_ref[:, low:high], put, span, pad, width)

    turned = jnp.dot(wide_ref[...], basis_ref[...], preferred_element_type=F32)
    out_ref[...] = turned.astype(BF16).T


def rotate(gradients, basis, span, pad):
    rows, grads, width = gradients.shape
    wide = basis.shape[1]
    tile = 256
    return pl.pallas_call(
        functools.partial(rotate_kernel, rows, grads, span, pad, width),
        grid=(wide // tile,),
        out_shape=jax.ShapeDtypeStruct((wide, rows * grads), BF16),
        in_specs=[
            pl.BlockSpec(memory_space=pl.ANY),
            pl.BlockSpec((wide, tile), lambda n: (0, n)),
        ],
        out_specs=pl.BlockSpec((tile, rows * grads), lambda n: (n, 0)),
        scratch_shapes=[
            pltpu.VMEM((rows * grads, width), F32),
            pltpu.VMEM((rows * grads, LANE), F32),
            pltpu.VMEM((rows * grads, width), BF16),
            pltpu.VMEM((rows * grads, wide), BF16),
            pltpu.SemaphoreType.DMA,
        ],
        compiler_params=pltpu.CompilerParams(vmem_limit_bytes=56 << 20),
    )(gradients.reshape(rows * grads, width), basis)


def finish_kernel(grads, span, pad, group, moved_ref, basis_ref, seed_ref, out_ref, eigen_ref, turned_ref):
    rows = LANE // group
    sources = moved_ref.shape[0]

    @pl.when(pl.program_id(0) == 0)
    def _():
        side = group * LANE
        source = lax.broadcasted_iota(jnp.int32, (side, side), 0)
        target = lax.broadcasted_iota(jnp.int32, (side, side), 1)
        inner = source & (rows - 1)
        chunk = lax.shift_right_logical(source & (LANE - 1), rows.bit_length() - 1)
        outer = lax.shift_right_logical(source, LANE.bit_length() - 1)
        swap = (target == chunk * LANE + outer * rows + inner).astype(F32).astype(BF16)
        tiles = grads // group

        def gather(block, carry):
            parts = []
            for tile in range(tiles):
                parts.append(
                    jnp.concatenate(
                        [
                            moved_ref[block * group + s, :, tile * LANE : (tile + 1) * LANE]
                            for s in range(group)
                        ],
                        axis=1,
                    )
                )
            swapped = jnp.dot(jnp.concatenate(parts, axis=0), swap, preferred_element_type=F32).astype(BF16)
            at = pl.ds(pl.multiple_of(block * LANE, LANE), LANE)
            for tile in range(tiles):
                for c in range(group):
                    g = tile * group + c
                    eigen_ref[g * pad : (g + 1) * pad, at] = swapped[
                        tile * pad : (tile + 1) * pad, c * LANE : (c + 1) * LANE
                    ]
            return carry

        lax.fori_loop(0, sources // group, gather, 0)
        turned_ref[...] = jnp.zeros_like(turned_ref)

    both = jnp.dot(eigen_ref[...], basis_ref[...], preferred_element_type=F32)
    value = jnp.exp2(seed_ref[...].astype(F32) * 0.125 - 4.0)
    denom = value + 0.1
    for g in range(grads):
        turned_ref[pl.ds(g, span, stride=grads), :] = both[g * pad : g * pad + span, :] / denom
    out_ref[...] = turned_ref[...].T[:, : span * grads]


def finish(moved, basis, seeds, grads):
    span, pad = seeds.shape[0], moved.shape[1]
    width = basis.shape[0]
    rows = width // moved.shape[0]
    tile = 128
    return pl.pallas_call(
        functools.partial(finish_kernel, grads, span, pad, LANE // rows),
        grid=(width // tile,),
        out_shape=jax.ShapeDtypeStruct((width, span * grads), F32),
        in_specs=[
            pl.BlockSpec(memory_space=pltpu.VMEM),
            pl.BlockSpec((width, tile), lambda n: (0, n)),
            pl.BlockSpec((span, tile), lambda n: (0, n)),
        ],
        out_specs=pl.BlockSpec((tile, span * grads), lambda n: (n, 0)),
        scratch_shapes=[
            pltpu.VMEM((pad * grads, width), BF16),
            pltpu.VMEM((up(span * grads, LANE), tile), F32),
        ],
        compiler_params=pltpu.CompilerParams(vmem_limit_bytes=56 << 20),
    )(moved, basis, seeds)


def local(gradients, in_basis, out_basis, eigen_seeds):
    devices = lax.axis_size("rows")
    rows, grads, width = gradients.shape
    span = in_basis.shape[0]
    pad = up(span, 16)
    shard = pad_shard(in_basis, pad)
    full_in = lax.all_gather(shard, "rows", axis=0, tiled=True)
    full_out = lax.all_gather(out_basis, "rows", axis=0, tiled=True)
    rotated = rotate(gradients, full_in, span, pad)
    rotated = rotated.reshape(devices, pad, rows * grads)
    moved = lax.all_to_all(rotated, "rows", split_axis=0, concat_axis=0, tiled=True)
    return finish(moved, full_out, eigen_seeds, grads)


def solution(mesh):
    placed = (
        P(("layer", "rows"), None, None),
        P(("layer", "rows"), None),
        P(("layer", "rows"), None),
        P(("layer", "rows"), None),
    )
    return jax.shard_map(
        local, mesh=mesh, in_specs=placed, out_specs=P("layer", "rows"), check_vma=False
    )
```

```python
import functools

import jax
import jax.numpy as jnp
import numpy as np
from jax import lax
from jax.experimental import pallas as pl
from jax.experimental.pallas import tpu as pltpu
from jax.sharding import PartitionSpec as P

LANE = 128
F32 = jnp.float32
BF16 = jnp.bfloat16
MESH = pl.DeviceIdType.MESH
Z, Y, X, CORE = 4, 2, 4, 2
PLANE = Y * X
DEVICES = Z * Y * X * CORE
HOPS = ((0, 0), (0, 1), (0, 3), (1, 0), (0, 2), (1, 1), (1, 3), (1, 2))


def up(value, step):
    return -(-value // step) * step


def device_of(kind, b, y, a):
    z = b * (1 - kind) + a * kind
    x = a * (1 - kind) + b * kind
    return ((z * Y + y) * X + x) * CORE + kind


def slot_of(kind, b, y, a):
    return ((kind * Z + b) * Y + y) * X + a


def wanted(owners, span, pad):
    table = np.full((len(owners), pad), -1, np.int32)
    for place, owner in enumerate(owners):
        table[place, :span] = owner * span + np.arange(span)
    return table.reshape(-1, 1, LANE)


def select(take, table, table_ref, tile):
    picks = table[tile, 0]
    tiles = sorted({int(p) // LANE for p in picks if p >= 0})
    want = jnp.broadcast_to(table_ref[tile], (LANE, LANE))
    row = lax.broadcasted_iota(jnp.int32, (LANE, LANE), 0)
    taken = [take(t) for t in tiles]
    chosen = [
        (want == row + t * LANE).astype(F32).astype(BF16)[: part.shape[1]] for t, part in zip(tiles, taken)
    ]
    moved = jnp.dot(
        jnp.concatenate(taken, axis=1), jnp.concatenate(chosen, axis=0), preferred_element_type=F32
    )
    return moved.astype(BF16)


def rotate_kernel(
    rows, grads, span, pad, width, in_table, col_table,
    shard_ref, low_out_ref, grad_ref, in_table_ref, col_table_ref,
    turned_ref, full_ref,
    units, own, raw, column, low_ref, wide_ref, total, stage,
    w_send, w_recv, o_send, o_recv, raw_sem, own_sem, stage_sem,
):
    me = lax.axis_index("rows")
    kind = me % CORE
    x = (me // CORE) % X
    y = (me // (CORE * X)) % Y
    z = me // (CORE * X * Y)
    a = x * (1 - kind) + z * kind
    b = z * (1 - kind) + x * kind
    other = me + 1 - 2 * kind
    ahead = device_of(kind, (b + 1) % Z, y, a)
    behind = device_of(kind, (b + 3) % Z, y, a)
    wide = pad * DEVICES

    def peer(p):
        dy, da = HOPS[p]
        return (y + dy) % Y, (a + da) % X

    fetch = pltpu.make_async_copy(grad_ref, raw, raw_sem)
    fetch.start()

    barrier = pltpu.get_barrier_semaphore()
    partners = [device_of(kind, b, *peer(p)) for p in range(1, PLANE)] + [ahead, behind, other]
    for partner in partners:
        pl.semaphore_signal(barrier, inc=1, device_id={"rows": partner}, device_id_type=MESH)

    mine = slot_of(kind, b, y, a)
    own[...] = jnp.zeros_like(own)
    for tile in range(wide // LANE):
        own[0:span, tile * LANE : (tile + 1) * LANE] = select(
            lambda t: shard_ref[:, t * LANE : (t + 1) * LANE], col_table, col_table_ref, tile
        )
    pl.semaphore_wait(barrier, len(partners))

    def send_unit(slot, target, source=None):
        pltpu.make_async_remote_copy(
            src_ref=units.at[slot] if source is None else source,
            dst_ref=units.at[slot],
            send_sem=w_send,
            recv_sem=w_recv.at[slot],
            device_id={"rows": target},
            device_id_type=MESH,
        ).start()

    def send_low(owner, target, source=None):
        pltpu.make_async_remote_copy(
            src_ref=full_ref.at[owner] if source is None else source,
            dst_ref=full_ref.at[owner],
            send_sem=o_send,
            recv_sem=o_recv.at[owner],
            device_id={"rows": target},
            device_id_type=MESH,
        ).start()

    def got_unit(slot):
        pltpu.make_async_copy(units.at[slot], units.at[slot], w_recv.at[slot]).wait()

    def got_low(owner):
        pltpu.make_async_copy(full_ref.at[owner], full_ref.at[owner], o_recv.at[owner]).wait()

    class Route:
        def __init__(self, name, send, got):
            self.name, self.send, self.got = name, send, got

        def start(self, source):
            place = self.name(kind, b, y, a)
            for target in [ahead, behind] + partners[: PLANE - 1] + [other]:
                self.send(place, target, source)

        def plane(self, p):
            place = self.name(kind, b, *peer(p))
            self.got(place)
            for target in (ahead, behind, other):
                self.send(place, target)

        def near(self, p):
            place = self.name(kind, (b + 3) % Z, *peer(p))
            self.got(place)
            if p % 2 == 0:
                self.send(place, ahead)
            self.send(place, other)
            place = self.name(kind, (b + 1) % Z, *peer(p))
            self.got(place)
            if p % 2 == 1:
                self.send(place, behind)
            self.send(place, other)

        def far(self, p):
            place = self.name(kind, (b + 2) % Z, *peer(p))
            self.got(place)
            self.send(place, other)

        def beside(self, step):
            for p in range(PLANE):
                dy, da = HOPS[p]
                self.got(self.name(1 - kind, (a + step) % Z, (y + dy) % Y, (b + da) % X))

    basis = Route(slot_of, send_unit, got_unit)
    lows = Route(device_of, send_low, got_low)

    basis.start(own)
    keep = pltpu.make_async_copy(own, units.at[mine], own_sem.at[0])
    keep.start()
    keep_low = pltpu.make_async_copy(low_out_ref, full_ref.at[me], own_sem.at[1])
    keep_low.start()

    fetch.wait()
    count = -(-width // LANE)
    low_ref[:, (count - 1) * LANE :] = jnp.zeros((rows * grads, LANE), BF16)

    def narrow(tile):
        left = tile * LANE
        now = min(LANE, width - left)
        column[:, 0:now] = raw[:, left : left + now]
        for g in range(grads):
            picked = column[pl.ds(g, rows, stride=grads), :].astype(BF16)
            low_ref[g * rows : (g + 1) * rows, left : left + now] = picked[:, 0:now]

    def widen(tile):
        wide_ref[:, tile * LANE : (tile + 1) * LANE] = select(
            lambda t: low_ref[:, t * LANE : (t + 1) * LANE], in_table, in_table_ref, tile
        )

    pieces = [functools.partial(narrow, t) for t in range(count)]
    pieces += [functools.partial(widen, t) for t in range(wide // LANE)]
    events = []
    for p in range(1, PLANE):
        events.append(functools.partial(basis.plane, p))
        events.append(functools.partial(basis.near, p - 1))
    for at, piece in enumerate(pieces):
        piece()
        done = at * len(events) // len(pieces)
        for event in events[done : (at + 1) * len(events) // len(pieces)]:
            event()
    basis.near(PLANE - 1)
    lows.start(low_out_ref)

    block = 256
    blocks = wide // block
    depth = PLANE * pad

    def part(step, n):
        at = pl.ds(pl.multiple_of(n * block, block), block)
        lefts, rights = [], []
        for what, where in ((kind, b), (1 - kind, a)):
            group = what * Z + (where + step) % Z
            lefts.append(wide_ref[:, pl.ds(pl.multiple_of(group * depth, LANE), depth)])
            rights.append(units[pl.ds(group * PLANE, PLANE), :, at].reshape(depth, block))
        return jnp.dot(
            jnp.concatenate(lefts, axis=1), jnp.concatenate(rights, axis=0), preferred_element_type=F32
        )

    def multiply(step, first, last):
        def body(n, carry):
            at = pl.ds(pl.multiple_of(n * block, block), block)
            if step == 0:
                total[:, at] = part(step, n)
            else:
                total[:, at] += part(step, n)
            return carry

        lax.fori_loop(first, last, body, 0)

    keep.wait()
    keep_low.wait()
    third = blocks // 3
    basis.beside(0)
    multiply(0, 0, third)
    lows.plane(1)
    multiply(0, third, 2 * third)
    lows.near(0)
    lows.plane(2)
    multiply(0, 2 * third, blocks)
    lows.near(1)
    lows.plane(3)
    basis.beside(1)
    multiply(1, 0, third)
    lows.near(2)
    lows.plane(4)
    multiply(1, third, 2 * third)
    lows.near(3)
    lows.plane(5)
    multiply(1, 2 * third, blocks)
    lows.near(4)
    lows.plane(6)
    basis.beside(3)
    multiply(3, 0, third)
    lows.near(5)
    lows.plane(7)
    multiply(3, third, 2 * third)
    lows.near(6)
    lows.near(7)
    multiply(3, 2 * third, blocks)
    for p in range(PLANE):
        basis.far(p)
    basis.beside(2)

    def out_copy(n):
        return pltpu.make_async_copy(
            stage.at[n % 2],
            turned_ref.at[pl.ds(pl.multiple_of(n * block, block), block)],
            stage_sem.at[n % 2],
        )

    def last(n, carry):
        at = pl.ds(pl.multiple_of(n * block, block), block)

        @pl.when(n >= 2)
        def _():
            out_copy(n - 2).wait()

        stage[n % 2] = (total[:, at] + part(2, n)).astype(BF16).T
        out_copy(n).start()
        return carry

    lax.fori_loop(0, third, last, 0)
    for p in range(PLANE // 2):
        lows.far(p)
    lax.fori_loop(third, 2 * third, last, 0)
    for p in range(PLANE // 2, PLANE):
        lows.far(p)
    lax.fori_loop(2 * third, blocks, last, 0)
    out_copy(blocks - 2).wait()
    out_copy(blocks - 1).wait()
    for step in range(Z):
        lows.beside(step)
    sends = PLANE + 2 + 3 * (PLANE - 1) + 3 * PLANE + PLANE
    pltpu.make_async_copy(units.at[pl.ds(0, sends)], units.at[pl.ds(0, sends)], w_send).wait()
    pltpu.make_async_copy(full_ref.at[pl.ds(0, sends)], full_ref.at[pl.ds(0, sends)], o_send).wait()


def rotate(gradients, shard, low_out, pad):
    rows, grads, width = gradients.shape
    span = shard.shape[0]
    wide = pad * DEVICES
    in_owners = [
        device_of(kind, b, y, a)
        for kind in range(CORE)
        for b in range(Z)
        for y in range(Y)
        for a in range(X)
    ]
    in_table = wanted(in_owners, span, pad)
    col_table = wanted(list(range(DEVICES)), span, pad)
    any_space = pl.BlockSpec(memory_space=pl.ANY)
    vmem = pl.BlockSpec(memory_space=pltpu.VMEM)
    block = 256
    return pl.pallas_call(
        functools.partial(rotate_kernel, rows, grads, span, pad, width, in_table, col_table),
        out_shape=(
            jax.ShapeDtypeStruct((wide, rows * grads), BF16),
            jax.ShapeDtypeStruct((DEVICES,) + low_out.shape, BF16),
        ),
        in_specs=[vmem, any_space, any_space, vmem, vmem],
        out_specs=(any_space, any_space),
        scratch_shapes=[
            pltpu.VMEM((DEVICES, pad, wide), BF16),
            pltpu.VMEM((pad, wide), BF16),
            pltpu.VMEM((rows * grads, width), F32),
            pltpu.VMEM((rows * grads, LANE), F32),
            pltpu.VMEM((rows * grads, up(width, LANE)), BF16),
            pltpu.VMEM((rows * grads, wide), BF16),
            pltpu.VMEM((rows * grads, wide), F32),
            pltpu.VMEM((2, block, rows * grads), BF16),
            pltpu.SemaphoreType.DMA,
            pltpu.SemaphoreType.DMA((DEVICES,)),
            pltpu.SemaphoreType.DMA,
            pltpu.SemaphoreType.DMA((DEVICES,)),
            pltpu.SemaphoreType.DMA,
            pltpu.SemaphoreType.DMA((2,)),
            pltpu.SemaphoreType.DMA((2,)),
        ],
        compiler_params=pltpu.CompilerParams(
            vmem_limit_bytes=60 << 20, collective_id=0, has_side_effects=True
        ),
    )(
        shard,
        low_out,
        gradients.reshape(rows * grads, width),
        jnp.asarray(in_table),
        jnp.asarray(col_table),
    )


def finish_kernel(grads, span, pad, group, moved_ref, basis_ref, seed_ref, out_ref, eigen_ref, ready, sem):
    rows = LANE // group
    sources = moved_ref.shape[0]
    step = pl.program_id(0)
    tile = basis_ref.shape[1]
    halves = tile // LANE

    @pl.when(step == 0)
    def _():
        side = group * LANE
        source = lax.broadcasted_iota(jnp.int32, (side, side), 0)
        target = lax.broadcasted_iota(jnp.int32, (side, side), 1)
        inner = source & (rows - 1)
        chunk = lax.shift_right_logical(source & (LANE - 1), rows.bit_length() - 1)
        outer = lax.shift_right_logical(source, LANE.bit_length() - 1)
        swap = (target == chunk * LANE + outer * rows + inner).astype(F32).astype(BF16)
        tiles = grads // group

        def gather(block, carry):
            parts = []
            for tile in range(tiles):
                parts.append(
                    jnp.concatenate(
                        [
                            moved_ref[block * group + s, :, tile * LANE : (tile + 1) * LANE]
                            for s in range(group)
                        ],
                        axis=1,
                    )
                )
            swapped = jnp.dot(jnp.concatenate(parts, axis=0), swap, preferred_element_type=F32).astype(BF16)
            at = pl.ds(pl.multiple_of(block * LANE, LANE), LANE)
            for tile in range(tiles):
                for c in range(group):
                    g = tile * group + c
                    eigen_ref[g * pad : (g + 1) * pad, at] = swapped[
                        tile * pad : (tile + 1) * pad, c * LANE : (c + 1) * LANE
                    ]
            return carry

        lax.fori_loop(0, sources // group, gather, 0)

    def out_copy(which, half):
        return pltpu.make_async_copy(
            ready.at[which % 2, half],
            out_ref.at[:, pl.ds(pl.multiple_of((which * halves + half) * LANE, LANE), LANE)],
            sem.at[which % 2, half],
        )

    @pl.when(step >= 2)
    def _():
        for half in range(halves):
            out_copy(step - 2, half).wait()

    value = jnp.exp2(seed_ref[...].astype(F32) * 0.125 - 4.0)
    denom = value + 0.1
    for g in range(0, grads, 8):
        both = jnp.dot(eigen_ref[g * pad : (g + 8) * pad, :], basis_ref[...], preferred_element_type=F32)
        for d in range(8):
            result = both[d * pad : d * pad + span, :] / denom
            for half in range(halves):
                ready[step % 2, half, pl.ds(g + d, span, stride=grads), :] = result[
                    :, half * LANE : (half + 1) * LANE
                ]
    for half in range(halves):
        out_copy(step, half).start()

    @pl.when(step == pl.num_programs(0) - 1)
    def _():
        for half in range(halves):
            out_copy(step - 1, half).wait()
            out_copy(step, half).wait()


def finish(moved, basis, seeds, grads):
    span, pad = seeds.shape[0], moved.shape[1]
    width = basis.shape[0]
    rows = width // moved.shape[0]
    tile = 256
    return pl.pallas_call(
        functools.partial(finish_kernel, grads, span, pad, LANE // rows),
        grid=(width // tile,),
        out_shape=jax.ShapeDtypeStruct((span * grads, width), F32),
        in_specs=[
            pl.BlockSpec(memory_space=pltpu.VMEM),
            pl.BlockSpec((width, tile), lambda n: (0, n)),
            pl.BlockSpec((span, tile), lambda n: (0, n)),
        ],
        out_specs=pl.BlockSpec(memory_space=pl.ANY),
        scratch_shapes=[
            pltpu.VMEM((pad * grads, width), BF16),
            pltpu.VMEM((2, tile // LANE, span * grads, LANE), F32),
            pltpu.SemaphoreType.DMA((2, tile // LANE)),
        ],
        compiler_params=pltpu.CompilerParams(vmem_limit_bytes=56 << 20),
    )(moved, basis, seeds)


def local(gradients, in_basis, out_basis, eigen_seeds):
    rows, grads, width = gradients.shape
    pad = up(in_basis.shape[0], 16)
    rotated, full_out = rotate(gradients, in_basis, out_basis, pad)
    rotated = rotated.reshape(DEVICES, pad, rows * grads)
    moved = lax.all_to_all(rotated, "rows", split_axis=0, concat_axis=0, tiled=True)
    full_out = full_out.reshape(-1, out_basis.shape[1])
    return finish(moved, full_out, eigen_seeds, grads).T


def solution(mesh):
    placed = (
        P(("layer", "rows"), None, None),
        P(("layer", "rows"), None),
        P(("layer", "rows"), None),
        P(("layer", "rows"), None),
    )
    return jax.shard_map(
        local, mesh=mesh, in_specs=placed, out_specs=P("layer", "rows"), check_vma=False
    )
```

```python
import functools

import jax
import jax.numpy as jnp
import numpy as np
from jax import lax
from jax.experimental import pallas as pl
from jax.experimental.pallas import tpu as pltpu
from jax.sharding import PartitionSpec as P

LANE = 128
F32 = jnp.float32
BF16 = jnp.bfloat16
MESH = pl.DeviceIdType.MESH
Z, Y, X, CORE = 4, 2, 4, 2
PLANE = Y * X
DEVICES = Z * Y * X * CORE
HOPS = ((0, 0), (1, 0), (0, 1), (0, 3), (1, 1), (1, 3), (0, 2), (1, 2))


def up(value, step):
    return -(-value // step) * step


def device_of(kind, b, y, a):
    z = b * (1 - kind) + a * kind
    x = a * (1 - kind) + b * kind
    return ((z * Y + y) * X + x) * CORE + kind


def slot_of(kind, b, y, a):
    return ((kind * Z + b) * Y + y) * X + a


def wanted(owners, span, pad):
    table = np.full((len(owners), pad), -1, np.int32)
    for place, owner in enumerate(owners):
        table[place, :span] = owner * span + np.arange(span)
    return table.reshape(-1, 1, LANE)


def select(take, table, table_ref, tile):
    picks = table[tile, 0]
    tiles = sorted({int(p) // LANE for p in picks if p >= 0})
    want = jnp.broadcast_to(table_ref[tile], (LANE, LANE))
    row = lax.broadcasted_iota(jnp.int32, (LANE, LANE), 0)
    taken = [take(t) for t in tiles]
    chosen = [
        (want == row + t * LANE).astype(F32).astype(BF16)[: part.shape[1]] for t, part in zip(tiles, taken)
    ]
    moved = jnp.dot(
        jnp.concatenate(taken, axis=1), jnp.concatenate(chosen, axis=0), preferred_element_type=F32
    )
    return moved.astype(BF16)


def rotate_kernel(
    rows, grads, span, pad, width, in_table, col_table,
    shard_ref, low_out_ref, grad_ref, in_table_ref, col_table_ref,
    turned_ref, full_ref,
    units, own, raw, column, low_ref, wide_ref, total, stage,
    w_send, w_recv, o_send, o_recv, raw_sem, own_sem, stage_sem,
):
    me = lax.axis_index("rows")
    kind = me % CORE
    x = (me // CORE) % X
    y = (me // (CORE * X)) % Y
    z = me // (CORE * X * Y)
    a = x * (1 - kind) + z * kind
    b = z * (1 - kind) + x * kind
    other = me + 1 - 2 * kind
    ahead = device_of(kind, (b + 1) % Z, y, a)
    behind = device_of(kind, (b + 3) % Z, y, a)
    wide = pad * DEVICES

    def peer(p):
        dy, da = HOPS[p]
        return (y + dy) % Y, (a + da) % X

    fetch = pltpu.make_async_copy(grad_ref, raw, raw_sem)
    fetch.start()

    barrier = pltpu.get_barrier_semaphore()
    across = device_of(kind, b, 1 - y, a)
    right = device_of(kind, b, y, (a + 1) % X)
    left = device_of(kind, b, y, (a + 3) % X)
    partners = [ahead, behind, right, left, across, other]
    for partner in partners:
        pl.semaphore_signal(barrier, inc=1, device_id={"rows": partner}, device_id_type=MESH)

    def send_low(owner, target, source=None):
        pltpu.make_async_remote_copy(
            src_ref=full_ref.at[owner] if source is None else source,
            dst_ref=full_ref.at[owner],
            send_sem=o_send,
            recv_sem=o_recv.at[owner],
            device_id={"rows": target},
            device_id_type=MESH,
        ).start()

    pl.semaphore_wait(barrier, len(partners))
    for target in (right, left, ahead, behind, across, other):
        send_low(me, target, low_out_ref)
    keep_low = pltpu.make_async_copy(low_out_ref, full_ref.at[me], own_sem.at[1])
    keep_low.start()

    mine = slot_of(kind, b, y, a)
    own[...] = jnp.zeros_like(own)
    for tile in range(wide // LANE):
        own[0:span, tile * LANE : (tile + 1) * LANE] = select(
            lambda t: shard_ref[:, t * LANE : (t + 1) * LANE], col_table, col_table_ref, tile
        )

    def send_unit(slot, target, source=None):
        pltpu.make_async_remote_copy(
            src_ref=units.at[slot] if source is None else source,
            dst_ref=units.at[slot],
            send_sem=w_send,
            recv_sem=w_recv.at[slot],
            device_id={"rows": target},
            device_id_type=MESH,
        ).start()

    def got_unit(slot):
        pltpu.make_async_copy(units.at[slot], units.at[slot], w_recv.at[slot]).wait()

    def got_low(owner):
        pltpu.make_async_copy(full_ref.at[owner], full_ref.at[owner], o_recv.at[owner]).wait()

    def plane(p):
        place = slot_of(kind, b, *peer(p))
        got_unit(place)
        hop = HOPS[p]
        if hop in ((1, 0), (0, 3)):
            send_unit(place, right)
        if hop in ((1, 0), (1, 1)):
            send_unit(place, left)
        for target in (ahead, behind, other):
            send_unit(place, target)

    def near(p):
        place = slot_of(kind, (b + 3) % Z, *peer(p))
        got_unit(place)
        if p % 2 == 0:
            send_unit(place, ahead)
        send_unit(place, other)
        place = slot_of(kind, (b + 1) % Z, *peer(p))
        got_unit(place)
        if p % 2 == 1:
            send_unit(place, behind)
        send_unit(place, other)

    def far(p):
        place = slot_of(kind, (b + 2) % Z, *peer(p))
        got_unit(place)
        send_unit(place, other)

    def beside(step):
        for dy, da in HOPS:
            got_unit(slot_of(1 - kind, (a + step) % Z, (y + dy) % Y, (b + da) % X))

    def low_row(da):
        owner = device_of(kind, b, y, (a + da) % X)
        got_low(owner)
        if da == 3:
            send_low(owner, right)
        for target in (ahead, behind, across, other):
            send_low(owner, target)

    def low_near(da):
        owner = device_of(kind, (b + 3) % Z, y, (a + da) % X)
        got_low(owner)
        if da < 2:
            send_low(owner, ahead)
        for target in (across, other):
            send_low(owner, target)
        owner = device_of(kind, (b + 1) % Z, y, (a + da) % X)
        got_low(owner)
        if da >= 2:
            send_low(owner, behind)
        for target in (across, other):
            send_low(owner, target)

    def low_far(da):
        owner = device_of(kind, (b + 2) % Z, y, (a + da) % X)
        got_low(owner)
        for target in (across, other):
            send_low(owner, target)

    def low_across(db, da):
        owner = device_of(kind, (b + db) % Z, 1 - y, (a + da) % X)
        got_low(owner)
        send_low(owner, other)

    def low_beside():
        for db in range(Z):
            for dy in range(Y):
                for da in range(X):
                    got_low(device_of(1 - kind, (a + db) % Z, (y + dy) % Y, (b + da) % X))

    for target in (ahead, behind, right, left, across, other):
        send_unit(mine, target, own)
    keep = pltpu.make_async_copy(own, units.at[mine], own_sem.at[0])
    keep.start()

    fetch.wait()
    count = -(-width // LANE)
    low_ref[:, (count - 1) * LANE :] = jnp.zeros((rows * grads, LANE), BF16)

    def narrow(tile):
        left = tile * LANE
        now = min(LANE, width - left)
        column[:, 0:now] = raw[:, left : left + now]
        for g in range(grads):
            picked = column[pl.ds(g, rows, stride=grads), :].astype(BF16)
            low_ref[g * rows : (g + 1) * rows, left : left + now] = picked[:, 0:now]

    def widen(tile):
        wide_ref[:, tile * LANE : (tile + 1) * LANE] = select(
            lambda t: low_ref[:, t * LANE : (t + 1) * LANE], in_table, in_table_ref, tile
        )

    pieces = [functools.partial(narrow, t) for t in range(count)]
    pieces += [functools.partial(widen, t) for t in range(wide // LANE)]
    step = functools.partial
    events = [
        step(low_row, 3), step(low_row, 1), step(plane, 1), step(low_near, 0), step(plane, 2), step(plane, 3),
        step(near, 0), step(low_row, 2), step(low_near, 3), step(plane, 4), step(plane, 5), step(low_near, 1),
        step(near, 1), step(low_near, 2), step(plane, 6), step(near, 2), step(plane, 7), step(near, 3),
    ]
    for at, piece in enumerate(pieces):
        piece()
        done = at * len(events) // len(pieces)
        for event in events[done : (at + 1) * len(events) // len(pieces)]:
            event()

    block = 256
    blocks = wide // block
    depth = PLANE * pad

    def part(step, n):
        at = pl.ds(pl.multiple_of(n * block, block), block)
        lefts, rights = [], []
        for what, where in ((kind, b), (1 - kind, a)):
            group = what * Z + (where + step) % Z
            lefts.append(wide_ref[:, pl.ds(pl.multiple_of(group * depth, LANE), depth)])
            rights.append(units[pl.ds(group * PLANE, PLANE), :, at].reshape(depth, block))
        return jnp.dot(
            jnp.concatenate(lefts, axis=1), jnp.concatenate(rights, axis=0), preferred_element_type=F32
        )

    def multiply(step, first, last):
        def body(n, carry):
            at = pl.ds(pl.multiple_of(n * block, block), block)
            if step == 0:
                total[:, at] = part(step, n)
            else:
                total[:, at] += part(step, n)
            return carry

        lax.fori_loop(first, last, body, 0)

    keep.wait()
    keep_low.wait()
    third = blocks // 3
    beside(0)
    multiply(0, 0, third)
    low_far(0)
    low_far(1)
    near(4)
    multiply(0, third, 2 * third)
    low_far(2)
    low_far(3)
    near(5)
    multiply(0, 2 * third, blocks)
    near(6)
    near(7)
    for da in range(X):
        low_across(0, da)
    beside(1)
    multiply(1, 0, third)
    far(0)
    multiply(1, third, 2 * third)
    far(1)
    multiply(1, 2 * third, blocks)
    far(2)
    for da in range(X):
        low_across(3, da)
    beside(3)
    multiply(3, 0, third)
    far(3)
    multiply(3, third, 2 * third)
    far(4)
    multiply(3, 2 * third, blocks)
    far(5)
    for da in range(X):
        low_across(1, da)
    far(6)
    far(7)
    beside(2)

    def out_copy(n):
        return pltpu.make_async_copy(
            stage.at[n % 2],
            turned_ref.at[pl.ds(pl.multiple_of(n * block, block), block)],
            stage_sem.at[n % 2],
        )

    def last(n, carry):
        at = pl.ds(pl.multiple_of(n * block, block), block)

        @pl.when(n >= 2)
        def _():
            out_copy(n - 2).wait()

        stage[n % 2] = (total[:, at] + part(2, n)).astype(BF16).T
        out_copy(n).start()
        return carry

    lax.fori_loop(0, third, last, 0)
    for da in range(X):
        low_across(2, da)
    lax.fori_loop(third, blocks, last, 0)
    out_copy(blocks - 2).wait()
    out_copy(blocks - 1).wait()
    low_beside()
    sends = 6 + 4 + 3 * (PLANE - 1) + 3 * PLANE + PLANE
    pltpu.make_async_copy(units.at[pl.ds(0, sends)], units.at[pl.ds(0, sends)], w_send).wait()
    lows = 6 + 1 + 4 * (X - 1) + 5 * X + 2 * X + Z * X
    pltpu.make_async_copy(full_ref.at[pl.ds(0, lows)], full_ref.at[pl.ds(0, lows)], o_send).wait()


def rotate(gradients, shard, low_out, pad):
    rows, grads, width = gradients.shape
    span = shard.shape[0]
    wide = pad * DEVICES
    in_owners = [
        device_of(kind, b, y, a)
        for kind in range(CORE)
        for b in range(Z)
        for y in range(Y)
        for a in range(X)
    ]
    in_table = wanted(in_owners, span, pad)
    col_table = wanted(list(range(DEVICES)), span, pad)
    any_space = pl.BlockSpec(memory_space=pl.ANY)
    vmem = pl.BlockSpec(memory_space=pltpu.VMEM)
    block = 256
    return pl.pallas_call(
        functools.partial(rotate_kernel, rows, grads, span, pad, width, in_table, col_table),
        out_shape=(
            jax.ShapeDtypeStruct((wide, rows * grads), BF16),
            jax.ShapeDtypeStruct((DEVICES,) + low_out.shape, BF16),
        ),
        in_specs=[vmem, any_space, any_space, vmem, vmem],
        out_specs=(any_space, any_space),
        scratch_shapes=[
            pltpu.VMEM((DEVICES, pad, wide), BF16),
            pltpu.VMEM((pad, wide), BF16),
            pltpu.VMEM((rows * grads, width), F32),
            pltpu.VMEM((rows * grads, LANE), F32),
            pltpu.VMEM((rows * grads, up(width, LANE)), BF16),
            pltpu.VMEM((rows * grads, wide), BF16),
            pltpu.VMEM((rows * grads, wide), F32),
            pltpu.VMEM((2, block, rows * grads), BF16),
            pltpu.SemaphoreType.DMA,
            pltpu.SemaphoreType.DMA((DEVICES,)),
            pltpu.SemaphoreType.DMA,
            pltpu.SemaphoreType.DMA((DEVICES,)),
            pltpu.SemaphoreType.DMA,
            pltpu.SemaphoreType.DMA((2,)),
            pltpu.SemaphoreType.DMA((2,)),
        ],
        compiler_params=pltpu.CompilerParams(
            vmem_limit_bytes=60 << 20, collective_id=0, has_side_effects=True
        ),
    )(
        shard,
        low_out,
        gradients.reshape(rows * grads, width),
        jnp.asarray(in_table),
        jnp.asarray(col_table),
    )


def finish_kernel(grads, span, pad, group, moved_ref, basis_ref, seed_ref, out_ref, eigen_ref, ready, sem):
    rows = LANE // group
    sources = moved_ref.shape[0]
    step = pl.program_id(0)
    tile = basis_ref.shape[1]
    halves = tile // LANE

    @pl.when(step == 0)
    def _():
        side = group * LANE
        source = lax.broadcasted_iota(jnp.int32, (side, side), 0)
        target = lax.broadcasted_iota(jnp.int32, (side, side), 1)
        inner = source & (rows - 1)
        chunk = lax.shift_right_logical(source & (LANE - 1), rows.bit_length() - 1)
        outer = lax.shift_right_logical(source, LANE.bit_length() - 1)
        swap = (target == chunk * LANE + outer * rows + inner).astype(F32).astype(BF16)
        tiles = grads // group

        def gather(block, carry):
            parts = []
            for tile in range(tiles):
                parts.append(
                    jnp.concatenate(
                        [
                            moved_ref[block * group + s, :, tile * LANE : (tile + 1) * LANE]
                            for s in range(group)
                        ],
                        axis=1,
                    )
                )
            swapped = jnp.dot(jnp.concatenate(parts, axis=0), swap, preferred_element_type=F32).astype(BF16)
            at = pl.ds(pl.multiple_of(block * LANE, LANE), LANE)
            for tile in range(tiles):
                for c in range(group):
                    g = tile * group + c
                    eigen_ref[g * pad : (g + 1) * pad, at] = swapped[
                        tile * pad : (tile + 1) * pad, c * LANE : (c + 1) * LANE
                    ]
            return carry

        lax.fori_loop(0, sources // group, gather, 0)

    def out_copy(which, half):
        return pltpu.make_async_copy(
            ready.at[which % 2, half],
            out_ref.at[:, pl.ds(pl.multiple_of((which * halves + half) * LANE, LANE), LANE)],
            sem.at[which % 2, half],
        )

    @pl.when(step >= 2)
    def _():
        for half in range(halves):
            out_copy(step - 2, half).wait()

    value = jnp.exp2(seed_ref[...].astype(F32) * 0.125 - 4.0)
    denom = value + 0.1
    for g in range(0, grads, 8):
        both = jnp.dot(eigen_ref[g * pad : (g + 8) * pad, :], basis_ref[...], preferred_element_type=F32)
        for d in range(8):
            result = both[d * pad : d * pad + span, :] / denom
            for half in range(halves):
                ready[step % 2, half, pl.ds(g + d, span, stride=grads), :] = result[
                    :, half * LANE : (half + 1) * LANE
                ]
    for half in range(halves):
        out_copy(step, half).start()

    @pl.when(step == pl.num_programs(0) - 1)
    def _():
        for half in range(halves):
            out_copy(step - 1, half).wait()
            out_copy(step, half).wait()


def finish(moved, basis, seeds, grads):
    span, pad = seeds.shape[0], moved.shape[1]
    width = basis.shape[0]
    rows = width // moved.shape[0]
    tile = 256
    return pl.pallas_call(
        functools.partial(finish_kernel, grads, span, pad, LANE // rows),
        grid=(width // tile,),
        out_shape=jax.ShapeDtypeStruct((span * grads, width), F32),
        in_specs=[
            pl.BlockSpec(memory_space=pltpu.VMEM),
            pl.BlockSpec((width, tile), lambda n: (0, n)),
            pl.BlockSpec((span, tile), lambda n: (0, n)),
        ],
        out_specs=pl.BlockSpec(memory_space=pl.ANY),
        scratch_shapes=[
            pltpu.VMEM((pad * grads, width), BF16),
            pltpu.VMEM((2, tile // LANE, span * grads, LANE), F32),
            pltpu.SemaphoreType.DMA((2, tile // LANE)),
        ],
        compiler_params=pltpu.CompilerParams(vmem_limit_bytes=56 << 20),
    )(moved, basis, seeds)


def local(gradients, in_basis, out_basis, eigen_seeds):
    rows, grads, width = gradients.shape
    pad = up(in_basis.shape[0], 16)
    rotated, full_out = rotate(gradients, in_basis, out_basis, pad)
    rotated = rotated.reshape(DEVICES, pad, rows * grads)
    moved = lax.all_to_all(rotated, "rows", split_axis=0, concat_axis=0, tiled=True)
    full_out = full_out.reshape(-1, out_basis.shape[1])
    return finish(moved, full_out, eigen_seeds, grads).T


def solution(mesh):
    placed = (
        P(("layer", "rows"), None, None),
        P(("layer", "rows"), None),
        P(("layer", "rows"), None),
        P(("layer", "rows"), None),
    )
    return jax.shard_map(
        local, mesh=mesh, in_specs=placed, out_specs=P("layer", "rows"), check_vma=False
    )
```

```python
import functools

import jax
import jax.numpy as jnp
import numpy as np
from jax import lax
from jax.experimental import pallas as pl
from jax.experimental.pallas import tpu as pltpu
from jax.sharding import PartitionSpec as P

LANE = 128
F32 = jnp.float32
BF16 = jnp.bfloat16
MESH = pl.DeviceIdType.MESH
Z, Y, X, CORE = 4, 2, 4, 2
PLANE = Y * X
DEVICES = Z * Y * X * CORE
HOPS = ((0, 0), (1, 0), (0, 1), (0, 3), (1, 1), (1, 3), (0, 2), (1, 2))


def up(value, step):
    return -(-value // step) * step


def device_of(kind, b, y, a):
    z = b * (1 - kind) + a * kind
    x = a * (1 - kind) + b * kind
    return ((z * Y + y) * X + x) * CORE + kind


def slot_of(kind, b, y, a):
    return ((kind * Z + b) * Y + y) * X + a


def wanted(owners, span, pad):
    table = np.full((len(owners), pad), -1, np.int32)
    for place, owner in enumerate(owners):
        table[place, :span] = owner * span + np.arange(span)
    return table.reshape(-1, 1, LANE)


def select(take, table, table_ref, tile):
    picks = table[tile, 0]
    tiles = sorted({int(p) // LANE for p in picks if p >= 0})
    want = jnp.broadcast_to(table_ref[tile], (LANE, LANE))
    row = lax.broadcasted_iota(jnp.int32, (LANE, LANE), 0)
    taken = [take(t) for t in tiles]
    chosen = [
        (want == row + t * LANE).astype(F32).astype(BF16)[: part.shape[1]] for t, part in zip(tiles, taken)
    ]
    moved = jnp.dot(
        jnp.concatenate(taken, axis=1), jnp.concatenate(chosen, axis=0), preferred_element_type=F32
    )
    return moved.astype(BF16)


def rotate_kernel(
    rows, grads, span, pad, width, in_table, col_table,
    shard_ref, low_out_ref, grad_ref, in_table_ref, col_table_ref,
    turned_ref, full_ref,
    units, own, raw, column, low_ref, wide_ref, total, spread, stage,
    w_send, w_recv, o_send, o_recv, raw_sem, own_sem, stage_sem,
):
    me = lax.axis_index("rows")
    kind = me % CORE
    x = (me // CORE) % X
    y = (me // (CORE * X)) % Y
    z = me // (CORE * X * Y)
    a = x * (1 - kind) + z * kind
    b = z * (1 - kind) + x * kind
    other = me + 1 - 2 * kind
    ahead = device_of(kind, (b + 1) % Z, y, a)
    behind = device_of(kind, (b + 3) % Z, y, a)
    wide = pad * DEVICES

    def peer(p):
        dy, da = HOPS[p]
        return (y + dy) % Y, (a + da) % X

    part_rows = raw.shape[0] // grads

    def fetch(part):
        return pltpu.make_async_copy(grad_ref.at[pl.ds(part * raw.shape[0], raw.shape[0])], raw, raw_sem)

    fetch(0).start()

    barrier = pltpu.get_barrier_semaphore()
    across = device_of(kind, b, 1 - y, a)
    right = device_of(kind, b, y, (a + 1) % X)
    left = device_of(kind, b, y, (a + 3) % X)
    partners = [ahead, behind, right, left, across, other]
    for partner in partners:
        pl.semaphore_signal(barrier, inc=1, device_id={"rows": partner}, device_id_type=MESH)

    def send_low(owner, target, source=None):
        pltpu.make_async_remote_copy(
            src_ref=full_ref.at[owner] if source is None else source,
            dst_ref=full_ref.at[owner],
            send_sem=o_send,
            recv_sem=o_recv.at[owner],
            device_id={"rows": target},
            device_id_type=MESH,
        ).start()

    pl.semaphore_wait(barrier, len(partners))
    for target in (right, left, ahead, behind, across, other):
        send_low(me, target, low_out_ref)
    keep_low = pltpu.make_async_copy(low_out_ref, full_ref.at[me], own_sem.at[1])
    keep_low.start()

    mine = slot_of(kind, b, y, a)
    own[...] = jnp.zeros_like(own)
    for tile in range(wide // LANE):
        own[0:span, tile * LANE : (tile + 1) * LANE] = select(
            lambda t: shard_ref[:, t * LANE : (t + 1) * LANE], col_table, col_table_ref, tile
        )

    def send_unit(slot, target, source=None):
        pltpu.make_async_remote_copy(
            src_ref=units.at[slot] if source is None else source,
            dst_ref=units.at[slot],
            send_sem=w_send,
            recv_sem=w_recv.at[slot],
            device_id={"rows": target},
            device_id_type=MESH,
        ).start()

    def got_unit(slot):
        pltpu.make_async_copy(units.at[slot], units.at[slot], w_recv.at[slot]).wait()

    def got_low(owner):
        pltpu.make_async_copy(full_ref.at[owner], full_ref.at[owner], o_recv.at[owner]).wait()

    def plane(p):
        place = slot_of(kind, b, *peer(p))
        got_unit(place)
        hop = HOPS[p]
        if hop in ((1, 0), (0, 3)):
            send_unit(place, right)
        if hop in ((1, 0), (1, 1)):
            send_unit(place, left)
        for target in (ahead, behind, other):
            send_unit(place, target)

    def near(p):
        place = slot_of(kind, (b + 3) % Z, *peer(p))
        got_unit(place)
        if p % 2 == 0:
            send_unit(place, ahead)
        send_unit(place, other)
        place = slot_of(kind, (b + 1) % Z, *peer(p))
        got_unit(place)
        if p % 2 == 1:
            send_unit(place, behind)
        send_unit(place, other)

    def far(p):
        place = slot_of(kind, (b + 2) % Z, *peer(p))
        got_unit(place)
        send_unit(place, other)

    def beside(step):
        for dy, da in HOPS:
            got_unit(slot_of(1 - kind, (a + step) % Z, (y + dy) % Y, (b + da) % X))

    def low_row(da):
        owner = device_of(kind, b, y, (a + da) % X)
        got_low(owner)
        if da == 3:
            send_low(owner, right)
        for target in (ahead, behind, across, other):
            send_low(owner, target)

    def low_near(da):
        owner = device_of(kind, (b + 3) % Z, y, (a + da) % X)
        got_low(owner)
        if da < 2:
            send_low(owner, ahead)
        for target in (across, other):
            send_low(owner, target)
        owner = device_of(kind, (b + 1) % Z, y, (a + da) % X)
        got_low(owner)
        if da >= 2:
            send_low(owner, behind)
        for target in (across, other):
            send_low(owner, target)

    def low_far(da):
        owner = device_of(kind, (b + 2) % Z, y, (a + da) % X)
        got_low(owner)
        for target in (across, other):
            send_low(owner, target)

    def low_across(db, da):
        owner = device_of(kind, (b + db) % Z, 1 - y, (a + da) % X)
        got_low(owner)
        send_low(owner, other)

    def low_beside():
        for db in range(Z):
            for dy in range(Y):
                for da in range(X):
                    got_low(device_of(1 - kind, (a + db) % Z, (y + dy) % Y, (b + da) % X))

    for target in (ahead, behind, right, left, across, other):
        send_unit(mine, target, own)
    keep = pltpu.make_async_copy(own, units.at[mine], own_sem.at[0])
    keep.start()

    count = -(-width // LANE)
    low_ref[:, (count - 1) * LANE :] = jnp.zeros((rows * grads, LANE), BF16)

    def narrow(part, tile):
        if tile == 0:
            fetch(part).wait()
        left = tile * LANE
        now = min(LANE, width - left)
        column[:, 0:now] = raw[:, left : left + now]
        for g in range(grads):
            picked = column[pl.ds(g, part_rows, stride=grads), :].astype(BF16)
            at = g * rows + part * part_rows
            low_ref[at : at + part_rows, left : left + now] = picked[:, 0:now]
        if tile == count - 1 and part < rows // part_rows - 1:
            fetch(part + 1).start()

    def widen(tile):
        wide_ref[:, tile * LANE : (tile + 1) * LANE] = select(
            lambda t: low_ref[:, t * LANE : (t + 1) * LANE], in_table, in_table_ref, tile
        )

    pieces = [functools.partial(narrow, part, t) for part in range(rows // part_rows) for t in range(count)]
    pieces += [functools.partial(widen, t) for t in range(wide // LANE)]
    step = functools.partial
    events = [
        step(low_row, 3), step(low_row, 1), step(plane, 1), step(low_near, 0), step(plane, 2), step(plane, 3),
        step(near, 0), step(low_row, 2), step(low_near, 3), step(plane, 4), step(plane, 5), step(low_near, 1),
        step(near, 1), step(low_near, 2), step(plane, 6), step(near, 2), step(plane, 7), step(near, 3),
        step(low_far, 0), step(low_far, 1), step(near, 4), step(low_far, 2), step(low_far, 3), step(near, 5),
        step(near, 6), step(near, 7),
    ]
    for at, piece in enumerate(pieces):
        piece()
        done = at * len(events) // len(pieces)
        for event in events[done : (at + 1) * len(events) // len(pieces)]:
            event()

    block = 256
    blocks = wide // block
    depth = PLANE * pad

    def part(step, n):
        at = pl.ds(pl.multiple_of(n * block, block), block)
        lefts, rights = [], []
        for what, where in ((kind, b), (1 - kind, a)):
            group = what * Z + (where + step) % Z
            lefts.append(wide_ref[:, pl.ds(pl.multiple_of(group * depth, LANE), depth)])
            rights.append(units[pl.ds(group * PLANE, PLANE), :, at].reshape(depth, block))
        return jnp.dot(
            jnp.concatenate(lefts, axis=1), jnp.concatenate(rights, axis=0), preferred_element_type=F32
        )

    def multiply(step, first, last):
        def body(n, carry):
            at = pl.ds(pl.multiple_of(n * block, block), block)
            if step == 0:
                total[:, at] = part(step, n)
            else:
                total[:, at] += part(step, n)
            return carry

        lax.fori_loop(first, last, body, 0)

    keep.wait()
    keep_low.wait()
    third = blocks // 3
    beside(0)
    for da in range(X):
        low_across(0, da)
    for turn in range(3):
        multiply(0, turn * third, (turn + 1) * third)
        low_across(3, turn)
    far(0)
    low_across(3, 3)
    beside(1)
    for turn in range(3):
        multiply(1, turn * third, (turn + 1) * third)
        far(1 + turn)
    beside(3)
    for turn in range(3):
        multiply(3, turn * third, (turn + 1) * third)
        far(4 + turn)
    for da in range(X):
        low_across(1, da)
    far(7)
    beside(2)

    lanes = rows * grads // LANE
    many = stage.shape[1]
    batch = many * pad // block
    rounds = DEVICES // many

    def out_copy(n):
        return pltpu.make_async_copy(
            stage.at[n % 2],
            turned_ref.at[pl.ds(n * many, many)],
            stage_sem.at[n % 2],
        )

    def last(n, carry):
        for k in range(batch):
            part_n = n * batch + k
            at = pl.ds(pl.multiple_of(part_n * block, block), block)
            turned = (total[:, at] + part(2, part_n)).astype(BF16).T.astype(F32)
            for t in range(lanes):
                spread[pl.ds(k * block * lanes + t, block, stride=lanes), :] = turned[:, t * LANE : (t + 1) * LANE]

        @pl.when(n >= 2)
        def _():
            out_copy(n - 2).wait()

        for d in range(many):
            stage[n % 2, d] = spread[d * pad * lanes : (d * pad + span) * lanes, :].astype(BF16)
        out_copy(n).start()
        return carry

    lax.fori_loop(0, rounds, last, 0)
    for da in range(X):
        low_across(2, da)
    out_copy(rounds - 2).wait()
    out_copy(rounds - 1).wait()
    low_beside()
    sends = 6 + 4 + 3 * (PLANE - 1) + 3 * PLANE + PLANE
    pltpu.make_async_copy(units.at[pl.ds(0, sends)], units.at[pl.ds(0, sends)], w_send).wait()
    lows = 6 + 1 + 4 * (X - 1) + 5 * X + 2 * X + Z * X
    pltpu.make_async_copy(full_ref.at[pl.ds(0, lows)], full_ref.at[pl.ds(0, lows)], o_send).wait()


def rotate(gradients, shard, low_out, pad):
    rows, grads, width = gradients.shape
    span = shard.shape[0]
    wide = pad * DEVICES
    in_owners = [
        device_of(kind, b, y, a)
        for kind in range(CORE)
        for b in range(Z)
        for y in range(Y)
        for a in range(X)
    ]
    in_table = wanted(in_owners, span, pad)
    col_table = wanted(list(range(DEVICES)), span, pad)
    any_space = pl.BlockSpec(memory_space=pl.ANY)
    vmem = pl.BlockSpec(memory_space=pltpu.VMEM)
    lanes = rows * grads // LANE
    many = 16
    return pl.pallas_call(
        functools.partial(rotate_kernel, rows, grads, span, pad, width, in_table, col_table),
        out_shape=(
            jax.ShapeDtypeStruct((DEVICES, span * lanes, LANE), BF16),
            jax.ShapeDtypeStruct((DEVICES,) + low_out.shape, BF16),
        ),
        in_specs=[vmem, any_space, any_space, vmem, vmem],
        out_specs=(any_space, any_space),
        scratch_shapes=[
            pltpu.VMEM((DEVICES, pad, wide), BF16),
            pltpu.VMEM((pad, wide), BF16),
            pltpu.VMEM((rows * grads // 2, width), F32),
            pltpu.VMEM((rows * grads // 2, LANE), F32),
            pltpu.VMEM((rows * grads, up(width, LANE)), BF16),
            pltpu.VMEM((rows * grads, wide), BF16),
            pltpu.VMEM((rows * grads, wide), F32),
            pltpu.VMEM((many * pad * lanes, LANE), F32),
            pltpu.VMEM((2, many, span * lanes, LANE), BF16),
            pltpu.SemaphoreType.DMA,
            pltpu.SemaphoreType.DMA((DEVICES,)),
            pltpu.SemaphoreType.DMA,
            pltpu.SemaphoreType.DMA((DEVICES,)),
            pltpu.SemaphoreType.DMA,
            pltpu.SemaphoreType.DMA((2,)),
            pltpu.SemaphoreType.DMA((2,)),
        ],
        compiler_params=pltpu.CompilerParams(
            vmem_limit_bytes=60 << 20, collective_id=0, has_side_effects=True
        ),
    )(
        shard,
        low_out,
        gradients.reshape(rows * grads, width),
        jnp.asarray(in_table),
        jnp.asarray(col_table),
    )


def finish_kernel(grads, span, group, moved_ref, basis_ref, seed_ref, out_ref, eigen_ref, spread):
    rows = LANE // group
    sources, depth = moved_ref.shape[:2]

    @pl.when(pl.program_id(0) == 0)
    def _():
        side = group * LANE
        source = lax.broadcasted_iota(jnp.int32, (side, side), 0)
        target = lax.broadcasted_iota(jnp.int32, (side, side), 1)
        inner = source & (rows - 1)
        chunk = lax.shift_right_logical(source & (LANE - 1), rows.bit_length() - 1)
        outer = lax.shift_right_logical(source, LANE.bit_length() - 1)
        swap = (target == chunk * LANE + outer * rows + inner).astype(F32).astype(BF16)

        def gather(block, carry):
            parts = [moved_ref[block * group + s] for s in range(group)]
            swapped = jnp.dot(jnp.concatenate(parts, axis=1), swap, preferred_element_type=F32)
            for c in range(group):
                spread[pl.ds(c, depth, stride=group), :] = swapped[:, c * LANE : (c + 1) * LANE]
            at = pl.ds(pl.multiple_of(block * LANE, LANE), LANE)
            eigen_ref[:, at] = spread[...].astype(BF16)
            return carry

        lax.fori_loop(0, sources // group, gather, 0)

    value = jnp.exp2(seed_ref[...].astype(F32) * 0.125 - 4.0)
    factor = 1.0 / (value + 0.1)
    both = jnp.dot(eigen_ref[...], basis_ref[...], preferred_element_type=F32)
    for c in range(span):
        out_ref[c * grads : (c + 1) * grads, :] = both[c * grads : (c + 1) * grads, :] * factor[c : c + 1, :]


def finish(moved, basis, seeds, grads):
    span = seeds.shape[0]
    width = basis.shape[0]
    rows = width // moved.shape[0]
    tile = 256
    return pl.pallas_call(
        functools.partial(finish_kernel, grads, span, LANE // rows),
        grid=(width // tile,),
        out_shape=jax.ShapeDtypeStruct((span * grads, width), F32),
        in_specs=[
            pl.BlockSpec(memory_space=pltpu.VMEM),
            pl.BlockSpec((width, tile), lambda n: (0, n)),
            pl.BlockSpec((span, tile), lambda n: (0, n)),
        ],
        out_specs=pl.BlockSpec((span * grads, tile), lambda n: (0, n)),
        scratch_shapes=[
            pltpu.VMEM((span * grads, width), BF16),
            pltpu.VMEM((span * grads, LANE), F32),
        ],
        compiler_params=pltpu.CompilerParams(vmem_limit_bytes=56 << 20),
    )(moved, basis, seeds)


def local(gradients, in_basis, out_basis, eigen_seeds):
    rows, grads, width = gradients.shape
    pad = up(in_basis.shape[0], 16)
    rotated, full_out = rotate(gradients, in_basis, out_basis, pad)
    moved = lax.all_to_all(rotated, "rows", split_axis=0, concat_axis=0, tiled=True)
    full_out = full_out.reshape(-1, out_basis.shape[1])
    return finish(moved, full_out, eigen_seeds, grads).T


def solution(mesh):
    placed = (
        P(("layer", "rows"), None, None),
        P(("layer", "rows"), None),
        P(("layer", "rows"), None),
        P(("layer", "rows"), None),
    )
    return jax.shard_map(
        local, mesh=mesh, in_specs=placed, out_specs=P("layer", "rows"), check_vma=False
    )
```

```python
import functools

import jax
import jax.numpy as jnp
import numpy as np
from jax import lax
from jax.experimental import pallas as pl
from jax.experimental.pallas import tpu as pltpu
from jax.sharding import PartitionSpec as P

LANE = 128
F32 = jnp.float32
BF16 = jnp.bfloat16
MESH = pl.DeviceIdType.MESH
Z, Y, X, CORE = 4, 2, 4, 2
PLANE = Y * X
DEVICES = Z * Y * X * CORE
HOPS = ((0, 0), (1, 0), (0, 1), (0, 3), (1, 1), (1, 3), (0, 2), (1, 2))


def up(value, step):
    return -(-value // step) * step


def device_of(kind, b, y, a):
    z = b * (1 - kind) + a * kind
    x = a * (1 - kind) + b * kind
    return ((z * Y + y) * X + x) * CORE + kind


def slot_of(kind, b, y, a):
    return ((kind * Z + b) * Y + y) * X + a


def wanted(owners, span, pad):
    table = np.full((len(owners), pad), -1, np.int32)
    for place, owner in enumerate(owners):
        table[place, :span] = owner * span + np.arange(span)
    return table.reshape(-1, 1, LANE)


def select(take, table, table_ref, tile):
    picks = table[tile, 0]
    tiles = sorted({int(p) // LANE for p in picks if p >= 0})
    want = jnp.broadcast_to(table_ref[tile], (LANE, LANE))
    row = lax.broadcasted_iota(jnp.int32, (LANE, LANE), 0)
    taken = [take(t) for t in tiles]
    chosen = [
        (want == row + t * LANE).astype(F32).astype(BF16)[: part.shape[1]] for t, part in zip(tiles, taken)
    ]
    moved = jnp.dot(
        jnp.concatenate(taken, axis=1), jnp.concatenate(chosen, axis=0), preferred_element_type=F32
    )
    return moved.astype(BF16)


def rotate_kernel(
    rows, grads, span, pad, width, in_table, col_table,
    shard_ref, low_out_ref, grad_ref, in_table_ref, col_table_ref,
    turned_ref, full_ref,
    units, own, raw, column, low_ref, wide_ref, total, spread, stage,
    w_send, w_recv, o_send, o_recv, raw_sem, own_sem, stage_sem,
):
    me = lax.axis_index("rows")
    kind = me % CORE
    x = (me // CORE) % X
    y = (me // (CORE * X)) % Y
    z = me // (CORE * X * Y)
    a = x * (1 - kind) + z * kind
    b = z * (1 - kind) + x * kind
    other = me + 1 - 2 * kind
    ahead = device_of(kind, (b + 1) % Z, y, a)
    behind = device_of(kind, (b + 3) % Z, y, a)
    wide = pad * DEVICES

    def peer(p):
        dy, da = HOPS[p]
        return (y + dy) % Y, (a + da) % X

    part_rows = raw.shape[0] // grads

    def fetch(part):
        return pltpu.make_async_copy(grad_ref.at[pl.ds(part * raw.shape[0], raw.shape[0])], raw, raw_sem)

    fetch(0).start()

    barrier = pltpu.get_barrier_semaphore()
    across = device_of(kind, b, 1 - y, a)
    right = device_of(kind, b, y, (a + 1) % X)
    left = device_of(kind, b, y, (a + 3) % X)
    partners = [ahead, behind, right, left, across, other]
    for partner in partners:
        pl.semaphore_signal(barrier, inc=1, device_id={"rows": partner}, device_id_type=MESH)

    def send_low(owner, target, source=None):
        pltpu.make_async_remote_copy(
            src_ref=full_ref.at[owner] if source is None else source,
            dst_ref=full_ref.at[owner],
            send_sem=o_send,
            recv_sem=o_recv.at[owner],
            device_id={"rows": target},
            device_id_type=MESH,
        ).start()

    pl.semaphore_wait(barrier, len(partners))
    for target in (right, left, ahead, behind, across, other):
        send_low(me, target, low_out_ref)
    keep_low = pltpu.make_async_copy(low_out_ref, full_ref.at[me], own_sem.at[1])
    keep_low.start()

    mine = slot_of(kind, b, y, a)
    own[...] = jnp.zeros_like(own)
    for tile in range(wide // LANE):
        own[0:span, tile * LANE : (tile + 1) * LANE] = select(
            lambda t: shard_ref[:, t * LANE : (t + 1) * LANE], col_table, col_table_ref, tile
        )

    def send_unit(slot, target, source=None):
        pltpu.make_async_remote_copy(
            src_ref=units.at[slot] if source is None else source,
            dst_ref=units.at[slot],
            send_sem=w_send,
            recv_sem=w_recv.at[slot],
            device_id={"rows": target},
            device_id_type=MESH,
        ).start()

    def got_unit(slot):
        pltpu.make_async_copy(units.at[slot], units.at[slot], w_recv.at[slot]).wait()

    def got_low(owner):
        pltpu.make_async_copy(full_ref.at[owner], full_ref.at[owner], o_recv.at[owner]).wait()

    def plane(p):
        place = slot_of(kind, b, *peer(p))
        got_unit(place)
        hop = HOPS[p]
        if hop in ((1, 0), (0, 3)):
            send_unit(place, right)
        if hop in ((1, 0), (1, 1)):
            send_unit(place, left)
        for target in (ahead, behind, other):
            send_unit(place, target)

    def near(p):
        place = slot_of(kind, (b + 3) % Z, *peer(p))
        got_unit(place)
        if p % 2 == 0:
            send_unit(place, ahead)
        send_unit(place, other)
        place = slot_of(kind, (b + 1) % Z, *peer(p))
        got_unit(place)
        if p % 2 == 1:
            send_unit(place, behind)
        send_unit(place, other)

    def far(p):
        place = slot_of(kind, (b + 2) % Z, *peer(p))
        got_unit(place)
        send_unit(place, other)

    def beside(step):
        for dy, da in HOPS:
            got_unit(slot_of(1 - kind, (a + step) % Z, (y + dy) % Y, (b + da) % X))

    def low_row(da):
        owner = device_of(kind, b, y, (a + da) % X)
        got_low(owner)
        if da == 3:
            send_low(owner, right)
        for target in (ahead, behind, across, other):
            send_low(owner, target)

    def low_near(da):
        owner = device_of(kind, (b + 3) % Z, y, (a + da) % X)
        got_low(owner)
        if da < 2:
            send_low(owner, ahead)
        for target in (across, other):
            send_low(owner, target)
        owner = device_of(kind, (b + 1) % Z, y, (a + da) % X)
        got_low(owner)
        if da >= 2:
            send_low(owner, behind)
        for target in (across, other):
            send_low(owner, target)

    def low_far(da):
        owner = device_of(kind, (b + 2) % Z, y, (a + da) % X)
        got_low(owner)
        for target in (across, other):
            send_low(owner, target)

    def low_across(db, da):
        owner = device_of(kind, (b + db) % Z, 1 - y, (a + da) % X)
        got_low(owner)
        send_low(owner, other)

    def low_beside():
        for db in range(Z):
            for dy in range(Y):
                for da in range(X):
                    got_low(device_of(1 - kind, (a + db) % Z, (y + dy) % Y, (b + da) % X))

    for target in (ahead, behind, right, left, across, other):
        send_unit(mine, target, own)
    keep = pltpu.make_async_copy(own, units.at[mine], own_sem.at[0])
    keep.start()

    count = -(-width // LANE)
    low_ref[:, (count - 1) * LANE :] = jnp.zeros((rows * grads, LANE), BF16)

    def narrow(part, tile):
        if tile == 0:
            fetch(part).wait()
        left = tile * LANE
        now = min(LANE, width - left)
        column[:, 0:now] = raw[:, left : left + now]
        for g in range(grads):
            picked = column[pl.ds(g, part_rows, stride=grads), :].astype(BF16)
            at = g * rows + part * part_rows
            low_ref[at : at + part_rows, left : left + now] = picked[:, 0:now]
        if tile == count - 1 and part < rows // part_rows - 1:
            fetch(part + 1).start()

    def widen(tile):
        wide_ref[:, tile * LANE : (tile + 1) * LANE] = select(
            lambda t: low_ref[:, t * LANE : (t + 1) * LANE], in_table, in_table_ref, tile
        )

    pieces = [functools.partial(narrow, part, t) for part in range(rows // part_rows) for t in range(count)]
    pieces += [functools.partial(widen, t) for t in range(wide // LANE)]
    step = functools.partial
    events = [
        step(low_row, 3), step(low_row, 1), step(plane, 1), step(low_near, 0), step(plane, 2), step(plane, 3),
        step(low_row, 2), step(low_near, 3), step(plane, 4), step(plane, 5), step(low_near, 1), step(plane, 6),
        step(plane, 7), step(low_near, 2),
    ]
    for at, piece in enumerate(pieces):
        piece()
        done = at * len(events) // len(pieces)
        for event in events[done : (at + 1) * len(events) // len(pieces)]:
            event()

    block = 256
    blocks = wide // block
    depth = PLANE * pad

    def part(step, n):
        at = pl.ds(pl.multiple_of(n * block, block), block)
        lefts, rights = [], []
        for what, where in ((kind, b), (1 - kind, a)):
            group = what * Z + (where + step) % Z
            lefts.append(wide_ref[:, pl.ds(pl.multiple_of(group * depth, LANE), depth)])
            rights.append(units[pl.ds(group * PLANE, PLANE), :, at].reshape(depth, block))
        return jnp.dot(
            jnp.concatenate(lefts, axis=1), jnp.concatenate(rights, axis=0), preferred_element_type=F32
        )

    def multiply(step, first, last):
        def body(n, carry):
            at = pl.ds(pl.multiple_of(n * block, block), block)
            if step == 0:
                total[:, at] = part(step, n)
            else:
                total[:, at] += part(step, n)
            return carry

        lax.fori_loop(first, last, body, 0)

    keep.wait()
    keep_low.wait()
    near(0)
    near(1)
    low_far(0)
    near(2)
    low_far(1)
    beside(0)
    for turn in range(6):
        multiply(0, turn * blocks // 6, (turn + 1) * blocks // 6)
        if turn < 5:
            near(3 + turn)
        if turn < 2:
            low_far(2 + turn)
        elif turn < 6:
            low_across(0, turn - 2)
    beside(1)
    for turn in range(4):
        multiply(1, turn * blocks // 4, (turn + 1) * blocks // 4)
        far(turn)
        low_across(3, turn)
    beside(3)
    for turn in range(4):
        multiply(3, turn * blocks // 4, (turn + 1) * blocks // 4)
        low_across(1, turn)
        if turn < 3:
            far(4 + turn)
    far(7)
    beside(2)

    lanes = rows * grads // LANE
    many = stage.shape[1]
    batch = many * pad // block
    rounds = DEVICES // many

    def out_copy(n):
        return pltpu.make_async_copy(
            stage.at[n % 2],
            turned_ref.at[pl.ds(n * many, many)],
            stage_sem.at[n % 2],
        )

    def last(n, carry):
        for k in range(batch):
            part_n = n * batch + k
            at = pl.ds(pl.multiple_of(part_n * block, block), block)
            turned = (total[:, at] + part(2, part_n)).astype(BF16).T.astype(F32)
            for t in range(lanes):
                spread[pl.ds(k * block * lanes + t, block, stride=lanes), :] = turned[:, t * LANE : (t + 1) * LANE]

        @pl.when(n >= 2)
        def _():
            out_copy(n - 2).wait()

        for d in range(many):
            stage[n % 2, d] = spread[d * pad * lanes : (d * pad + span) * lanes, :].astype(BF16)
        out_copy(n).start()
        return carry

    lax.fori_loop(0, rounds, last, 0)
    for da in range(X):
        low_across(2, da)
    out_copy(rounds - 2).wait()
    out_copy(rounds - 1).wait()
    low_beside()
    sends = 6 + 4 + 3 * (PLANE - 1) + 3 * PLANE + PLANE
    pltpu.make_async_copy(units.at[pl.ds(0, sends)], units.at[pl.ds(0, sends)], w_send).wait()
    lows = 6 + 1 + 4 * (X - 1) + 5 * X + 2 * X + Z * X
    pltpu.make_async_copy(full_ref.at[pl.ds(0, lows)], full_ref.at[pl.ds(0, lows)], o_send).wait()


def rotate(gradients, shard, low_out, pad):
    rows, grads, width = gradients.shape
    span = shard.shape[0]
    wide = pad * DEVICES
    in_owners = [
        device_of(kind, b, y, a)
        for kind in range(CORE)
        for b in range(Z)
        for y in range(Y)
        for a in range(X)
    ]
    in_table = wanted(in_owners, span, pad)
    col_table = wanted(list(range(DEVICES)), span, pad)
    any_space = pl.BlockSpec(memory_space=pl.ANY)
    vmem = pl.BlockSpec(memory_space=pltpu.VMEM)
    lanes = rows * grads // LANE
    many = 16
    return pl.pallas_call(
        functools.partial(rotate_kernel, rows, grads, span, pad, width, in_table, col_table),
        out_shape=(
            jax.ShapeDtypeStruct((DEVICES, span * lanes, LANE), BF16),
            jax.ShapeDtypeStruct((DEVICES,) + low_out.shape, BF16),
        ),
        in_specs=[vmem, any_space, any_space, vmem, vmem],
        out_specs=(any_space, any_space),
        scratch_shapes=[
            pltpu.VMEM((DEVICES, pad, wide), BF16),
            pltpu.VMEM((pad, wide), BF16),
            pltpu.VMEM((rows * grads // 2, width), F32),
            pltpu.VMEM((rows * grads // 2, LANE), F32),
            pltpu.VMEM((rows * grads, up(width, LANE)), BF16),
            pltpu.VMEM((rows * grads, wide), BF16),
            pltpu.VMEM((rows * grads, wide), F32),
            pltpu.VMEM((many * pad * lanes, LANE), F32),
            pltpu.VMEM((2, many, span * lanes, LANE), BF16),
            pltpu.SemaphoreType.DMA,
            pltpu.SemaphoreType.DMA((DEVICES,)),
            pltpu.SemaphoreType.DMA,
            pltpu.SemaphoreType.DMA((DEVICES,)),
            pltpu.SemaphoreType.DMA,
            pltpu.SemaphoreType.DMA((2,)),
            pltpu.SemaphoreType.DMA((2,)),
        ],
        compiler_params=pltpu.CompilerParams(
            vmem_limit_bytes=60 << 20, collective_id=0, has_side_effects=True
        ),
    )(
        shard,
        low_out,
        gradients.reshape(rows * grads, width),
        jnp.asarray(in_table),
        jnp.asarray(col_table),
    )


def finish_kernel(grads, span, group, moved_ref, basis_ref, seed_ref, out_ref, eigen_ref, spread):
    rows = LANE // group
    sources, depth = moved_ref.shape[:2]

    @pl.when(pl.program_id(0) == 0)
    def _():
        side = group * LANE
        source = lax.broadcasted_iota(jnp.int32, (side, side), 0)
        target = lax.broadcasted_iota(jnp.int32, (side, side), 1)
        inner = source & (rows - 1)
        chunk = lax.shift_right_logical(source & (LANE - 1), rows.bit_length() - 1)
        outer = lax.shift_right_logical(source, LANE.bit_length() - 1)
        swap = (target == chunk * LANE + outer * rows + inner).astype(F32).astype(BF16)

        def gather(block, carry):
            parts = [moved_ref[block * group + s] for s in range(group)]
            swapped = jnp.dot(jnp.concatenate(parts, axis=1), swap, preferred_element_type=F32)
            for c in range(group):
                spread[pl.ds(c, depth, stride=group), :] = swapped[:, c * LANE : (c + 1) * LANE]
            at = pl.ds(pl.multiple_of(block * LANE, LANE), LANE)
            eigen_ref[:, at] = spread[...].astype(BF16)
            return carry

        lax.fori_loop(0, sources // group, gather, 0)

    value = jnp.exp2(seed_ref[...].astype(F32) * 0.125 - 4.0)
    factor = 1.0 / (value + 0.1)
    both = jnp.dot(eigen_ref[...], basis_ref[...], preferred_element_type=F32)
    for c in range(span):
        out_ref[c * grads : (c + 1) * grads, :] = both[c * grads : (c + 1) * grads, :] * factor[c : c + 1, :]


def finish(moved, basis, seeds, grads):
    span = seeds.shape[0]
    width = basis.shape[0]
    rows = width // moved.shape[0]
    tile = 256
    return pl.pallas_call(
        functools.partial(finish_kernel, grads, span, LANE // rows),
        grid=(width // tile,),
        out_shape=jax.ShapeDtypeStruct((span * grads, width), F32),
        in_specs=[
            pl.BlockSpec(memory_space=pltpu.VMEM),
            pl.BlockSpec((width, tile), lambda n: (0, n)),
            pl.BlockSpec((span, tile), lambda n: (0, n)),
        ],
        out_specs=pl.BlockSpec((span * grads, tile), lambda n: (0, n)),
        scratch_shapes=[
            pltpu.VMEM((span * grads, width), BF16),
            pltpu.VMEM((span * grads, LANE), F32),
        ],
        compiler_params=pltpu.CompilerParams(vmem_limit_bytes=56 << 20),
    )(moved, basis, seeds)


def local(gradients, in_basis, out_basis, eigen_seeds):
    rows, grads, width = gradients.shape
    pad = up(in_basis.shape[0], 16)
    rotated, full_out = rotate(gradients, in_basis, out_basis, pad)
    moved = lax.all_to_all(rotated, "rows", split_axis=0, concat_axis=0, tiled=True)
    full_out = full_out.reshape(-1, out_basis.shape[1])
    return finish(moved, full_out, eigen_seeds, grads).T


def solution(mesh):
    placed = (
        P(("layer", "rows"), None, None),
        P(("layer", "rows"), None),
        P(("layer", "rows"), None),
        P(("layer", "rows"), None),
    )
    return jax.shard_map(
        local, mesh=mesh, in_specs=placed, out_specs=P("layer", "rows"), check_vma=False
    )
```
